256 devices in a mesh: seq: 16 (over z_hi, x, core), chan: 16 (over y, z_lo).
Axes of the slice: x: 4, y: 4, z: 8 (z_hi: 2, z_lo: 4; z = z_hi * 4 + z_lo), core: 2. Of those that a mesh axis runs over, the one named last changes fastest.
Arguments:
- inputs: bfloat16 [768, 262144], P('chan', 'seq'), may hold values from -6 to 6
- kernel: bfloat16 [768, 512, 512], P('chan', 'seq'), may hold values from -6 to 6
- forward_one: bfloat16 [512, 512], replicated, may hold values from -0.25 to 0.25
- forward_two: bfloat16 [512, 512], replicated, may hold values from -0.25 to 0.25
- inverse_one: bfloat16 [512, 512], replicated, may hold values from -0.25 to 0.25
- inverse_two: bfloat16 [512, 512], replicated, may hold values from -0.25 to 0.25
- norm_gain: float32 [768], replicated, may hold values from 0.1 to 1.9
- w_gate: bfloat16 [1536, 768], P('chan'), may hold values from -0.21875 to 0.21875
- w_up: bfloat16 [1536, 768], P('chan'), may hold values from -0.21875 to 0.21875
- w_down: bfloat16 [1536, 768], P('chan'), may hold values from -0.15625 to 0.15625
Outputs:
- output: bfloat16 [768, 262144], P('chan', 'seq')
The draws below stay inside these ranges and needn't reach their ends.
All inputs are finite; a program needn't handle non-finite values.
Results may differ from the reference program's by a relative error of at most 0.0075.
Values may be sent and summed in bfloat16 or wider, within the bound.
No kernel may reach another device: no remote copies, remote signals or barrier semaphores. Data moves between devices by JAX's collectives and lax.ppermute only.
A program may use at most 128 MiB of HBM per device.

```python
import jax
import jax.numpy as jnp
from jax import lax

BLOCK = 512
CH = 768
FF = 1536
SEQ = 262144


def block_scale(stream_key, extent, cuts, least, top_value):
    loudness = 1.0
    for position, shards_of in cuts:
        heights = jax.random.uniform(jax.random.fold_in(jax.random.fold_in(stream_key, 6), position), (shards_of,), jnp.float32, least / len(cuts), top_value / len(cuts))
        loudness = loudness * jnp.repeat(jnp.exp(heights), extent[position] // shards_of).reshape((-1,) + (1,) * (len(extent) - 1 - position))
    return loudness


def gaussian(key, shape, width, most, split=(), dtype=jnp.bfloat16):
    drawn = jax.random.normal(key, shape, jnp.float32) * width
    if len(split) > 0:
        drawn = block_scale(key, shape, split, -0.22, 0.18) * drawn
    return jnp.clip(drawn, min=-most, max=most).astype(dtype)


def setup_inputs(seed: int = 0) -> dict:
    key_of = jax.random.split(jax.random.key(seed), 11)
    inputs = gaussian(key_of[0], (CH, SEQ), 1.0, 6.0, ((0, 16), (1, 16)))
    kernel = gaussian(key_of[1], (CH, BLOCK, BLOCK), 1.0, 6.0, ((0, 16), (1, 16)))
    forward_one = gaussian(key_of[2], (BLOCK, BLOCK), BLOCK ** -0.5, 0.25)
    forward_two = gaussian(key_of[3], (BLOCK, BLOCK), BLOCK ** -0.5, 0.25)
    inverse_one = gaussian(key_of[4], (BLOCK, BLOCK), BLOCK ** -0.5, 0.25)
    inverse_two = gaussian(key_of[5], (BLOCK, BLOCK), BLOCK ** -0.5, 0.25)
    norm_gain = jnp.clip(1.0 + 0.18 * jax.random.normal(key_of[6], (CH,), jnp.float32), 0.1, 1.9)
    w_gate = gaussian(key_of[7], (FF, CH), CH ** -0.5, 0.21875, ((0, 16),))
    w_up = gaussian(key_of[8], (FF, CH), CH ** -0.5, 0.21875, ((0, 16),))
    w_down = gaussian(key_of[9], (FF, CH), FF ** -0.5, 0.15625, ((0, 16),))
    return dict(inputs=inputs, kernel=kernel, forward_one=forward_one, forward_two=forward_two, inverse_one=inverse_one, inverse_two=inverse_two, norm_gain=norm_gain, w_gate=w_gate, w_up=w_up, w_down=w_down)


def mix_group(pieces, forward_one, forward_two, inverse_one, inverse_two):
    inputs_group, kernel_group = pieces
    count = inputs_group.shape[0]
    order = forward_one.shape[0]
    cube = inputs_group.reshape(count, order, order)
    first_section = jnp.einsum('cab,bk->cak', cube.astype(jnp.float32), forward_one.astype(jnp.float32)).astype(jnp.bfloat16)
    spectrum = jnp.einsum('cak,aj->ckj', first_section.astype(jnp.float32), forward_two.astype(jnp.float32))
    scaled = (spectrum * kernel_group.astype(jnp.float32)).astype(jnp.bfloat16)
    partial_inv = jnp.einsum('ckj,ji->cki', scaled.astype(jnp.float32), inverse_two.astype(jnp.float32)).astype(jnp.bfloat16)
    mixed_out = jnp.einsum('cki,km->cim', partial_inv.astype(jnp.float32), inverse_one.astype(jnp.float32))
    resid = (cube.astype(jnp.float32) + mixed_out).astype(jnp.bfloat16)
    return resid.reshape(count, order * order)

def mlp_block(stream_block, norm_gain, w_gate, w_up, w_down):
    stream = stream_block.astype(jnp.float32)
    mean_square = lax.optimization_barrier(jnp.mean(stream * stream, axis=0, keepdims=True))
    normed = (stream * lax.rsqrt(mean_square + 1e-05) * norm_gain[:, None]).astype(jnp.bfloat16)
    gate_part = jnp.dot(w_gate, normed, preferred_element_type=jnp.float32)
    up_part = jnp.dot(w_up, normed, preferred_element_type=jnp.float32)
    hidden = (jax.nn.gelu(gate_part, approximate=True) * up_part).astype(jnp.bfloat16)
    summed = jnp.dot(w_down.T, hidden, preferred_element_type=jnp.float32)
    return (stream + summed).astype(jnp.bfloat16)

def reference(inputs, kernel, forward_one, forward_two, inverse_one, inverse_two, norm_gain, w_gate, w_up, w_down):
    groups = 16
    per_group = CH // groups
    grouped_in = inputs.reshape(groups, per_group, SEQ)
    grouped_k = kernel.reshape(groups, per_group, BLOCK, BLOCK)
    resid = lax.map(lambda pieces: mix_group(pieces, forward_one, forward_two, inverse_one, inverse_two), (grouped_in, grouped_k))
    resid = resid.reshape(CH, BLOCK, BLOCK).transpose(1, 0, 2)
    outputs = lax.map(lambda blk: mlp_block(blk, norm_gain, w_gate, w_up, w_down), resid)
    return outputs.transpose(1, 0, 2).reshape(CH, SEQ)
```

```python
import functools

import jax
import jax.numpy as jnp
from jax import lax
from jax.experimental import pallas as pl
from jax.experimental.pallas import tpu as pltpu
from jax.sharding import Mesh
from jax.sharding import PartitionSpec as P

SEQ_AXES = ("zh", "x", "core")
CHAN_AXES = ("y", "zl")
F32 = jnp.float32
BF16 = jnp.bfloat16
NT = (((1,), (1,)), ((), ()))
NN = (((1,), (0,)), ((), ()))


def params(mib):
    return pltpu.CompilerParams(vmem_limit_bytes=mib << 20)


def whole(shape):
    return pl.BlockSpec(shape, lambda *_: (0,) * len(shape), pipeline_mode=pl.Buffered(1))


def swap_matrix(n):
    r = lax.broadcasted_iota(jnp.int32, (n * n, n * n), 0)
    c = lax.broadcasted_iota(jnp.int32, (n * n, n * n), 1)
    return ((r // n == c % n) & (r % n == c // n)).astype(F32).astype(BF16)


def chunk_matrix(n, width):
    size = n * n * width
    r = lax.broadcasted_iota(jnp.int32, (size, size), 0)
    c = lax.broadcasted_iota(jnp.int32, (size, size), 1)
    ri, rj, rl = r // (n * width), (r // width) % n, r % width
    ci, cj, cl = c // (n * width), (c // width) % n, c % width
    return ((ri == cj) & (rj == ci) & (rl == cl)).astype(F32).astype(BF16)


def dot(a, b, dims=NN):
    return lax.dot_general(a, b, dims, preferred_element_type=F32)


def section_kernel(x_ref, factor_ref, out_ref, swap, turned, rows):
    @pl.when(pl.program_id(0) == 0)
    def _():
        swap[...] = swap_matrix(16)
        turned[...] = factor_ref[...].astype(F32).T.astype(BF16)

    for half in range(2):
        stack = jnp.concatenate(
            [x_ref[:, (half * 16 + a) * 512 : (half * 16 + a + 1) * 512] for a in range(16)], axis=0
        )
        moved = dot(swap[...], stack).astype(BF16)
        for c in range(16):
            rows[c * 32 + half * 16 : c * 32 + half * 16 + 16, :] = moved[c * 16 : c * 16 + 16]
    out_ref[...] = dot(turned[...], rows[...], NT).astype(BF16)


def first_sections(inputs, forward_one):
    channels, positions = inputs.shape
    return pl.pallas_call(
        section_kernel,
        grid=(channels // 16,),
        in_specs=[pl.BlockSpec((16, positions), lambda g: (g, 0)), whole((512, 512))],
        out_specs=pl.BlockSpec((512, 512), lambda g: (0, g)),
        out_shape=jax.ShapeDtypeStruct((512, channels * 32), BF16),
        scratch_shapes=[
            pltpu.VMEM((256, 256), BF16),
            pltpu.VMEM((512, 512), BF16),
            pltpu.VMEM((512, 512), BF16),
        ],
        compiler_params=params(32),
        name="first_sections",
    )(inputs, forward_one)


def gather_rows(in_ref, chunks, rows):
    for tile in range(2):
        lanes = slice(tile * 128, tile * 128 + 128)
        stack = jnp.concatenate(
            [
                jnp.concatenate([in_ref[4 * g + i, :, lanes] for i in range(4)], axis=1)
                for g in range(4)
            ],
            axis=0,
        )
        moved = dot(stack, chunks[...]).astype(BF16)
        for j in range(4):
            for g in range(4):
                rows[(tile * 4 + j) * 32 : (tile * 4 + j) * 32 + 32, g * 128 : g * 128 + 128] = moved[
                    g * 32 : g * 32 + 32, j * 128 : j * 128 + 128
                ]


def spectrum_kernel(in_ref, kernel_ref, forward_ref, inverse_ref, out_ref, chunks, turned, rows):
    @pl.when(pl.program_id(0) == 0)
    def _():
        chunks[...] = chunk_matrix(4, 32)
        turned[...] = inverse_ref[...].astype(F32).T.astype(BF16)

    gather_rows(in_ref, chunks, rows)
    spectrum = dot(rows[...], forward_ref[...])
    scaled = (spectrum * kernel_ref[...].reshape(256, 512).astype(F32)).astype(BF16)
    out_ref[...] = dot(turned[...], scaled, NT).astype(BF16)


def partial_inverses(sections, kernel, forward_two, inverse_two):
    channels = kernel.shape[0]
    return pl.pallas_call(
        spectrum_kernel,
        grid=(channels // 8,),
        in_specs=[
            pl.BlockSpec((16, 32, 256), lambda g: (0, 0, g)),
            pl.BlockSpec((8, 32, 512), lambda g: (g, 0, 0)),
            whole((512, 512)),
            whole((512, 512)),
        ],
        out_specs=pl.BlockSpec((512, 256), lambda g: (0, g)),
        out_shape=jax.ShapeDtypeStruct((512, channels * 32), BF16),
        scratch_shapes=[
            pltpu.VMEM((512, 512), BF16),
            pltpu.VMEM((512, 512), BF16),
            pltpu.VMEM((256, 512), BF16),
        ],
        compiler_params=params(32),
        name="partial_inverses",
    )(sections, kernel, forward_two, inverse_two)


def resid_kernel(in_ref, x_ref, inverse_ref, out_ref, chunks, swap, rows, mixed):
    @pl.when(pl.program_id(0) == 0)
    def _():
        chunks[...] = chunk_matrix(4, 32)
        swap[...] = swap_matrix(16)

    for part in range(2):
        gather_rows(in_ref.at[:, :, part * 256 : part * 256 + 256], chunks, rows)
        mixed[part * 256 : part * 256 + 256, :] = dot(rows[...], inverse_ref[...])
    for half in range(2):
        stack = jnp.concatenate(
            [mixed[c * 32 + half * 16 : c * 32 + half * 16 + 16, :] for c in range(16)], axis=0
        )
        high = stack.astype(BF16)
        rest = stack - high.astype(F32)
        mid = rest.astype(BF16)
        low = (rest - mid.astype(F32)).astype(BF16)
        moved = dot(swap[...], high) + dot(swap[...], mid) + dot(swap[...], low)
        for a in range(16):
            i = half * 16 + a
            value = x_ref[:, i * 512 : i * 512 + 512].astype(F32) + moved[a * 16 : a * 16 + 16]
            out_ref[i // 2, :, (i % 2) * 512 : (i % 2) * 512 + 512] = value.astype(BF16)


def residuals(parts, inputs, inverse_one):
    channels, positions = inputs.shape
    return pl.pallas_call(
        resid_kernel,
        grid=(channels // 16,),
        in_specs=[
            pl.BlockSpec((16, 32, 512), lambda g: (0, 0, g)),
            pl.BlockSpec((16, positions), lambda g: (g, 0)),
            whole((512, 512)),
        ],
        out_specs=pl.BlockSpec((16, 16, 1024), lambda g: (0, g, 0)),
        out_shape=jax.ShapeDtypeStruct((16, channels, positions // 16), BF16),
        scratch_shapes=[
            pltpu.VMEM((512, 512), BF16),
            pltpu.VMEM((256, 256), BF16),
            pltpu.VMEM((256, 512), BF16),
            pltpu.VMEM((512, 512), F32),
        ],
        compiler_params=params(32),
        name="residuals",
    )(parts, inputs, inverse_one)


def mlp_kernel(x_ref, gain_ref, gate_ref, up_ref, down_ref, out_ref, turned):
    hidden_units, channels = gate_ref.shape
    width = x_ref.shape[2]

    @pl.when(pl.program_id(0) == 0)
    def _():
        for h in range(0, hidden_units, 256):
            turned[:, h : h + 256] = down_ref[h : h + 256, :].astype(F32).T.astype(BF16)

    stream = x_ref[...].reshape(channels, width).astype(F32)
    mean_square = jnp.mean(stream * stream, axis=0, keepdims=True)
    normed = (stream * lax.rsqrt(mean_square + 1e-05) * gain_ref[...]).astype(BF16)
    total = stream
    step = 512
    for h in range(0, hidden_units, step):
        gate_part = dot(gate_ref[h : h + step, :], normed)
        up_part = dot(up_ref[h : h + step, :], normed)
        curve = 0.7978845608 * (gate_part + 0.044715 * gate_part * gate_part * gate_part)
        hidden = (0.5 * gate_part * (1.0 + jnp.tanh(curve)) * up_part).astype(BF16)
        total = total + dot(turned[:, h : h + step], hidden)
    out_ref[...] = total.astype(BF16).reshape(out_ref.shape)


def mlp(tokens, norm_gain, weights):
    sources, channels_each, count = tokens.shape
    hidden_units = weights.shape[0]
    channels = sources * channels_each
    tile = 256
    weight = lambda w: pl.BlockSpec((hidden_units, channels), lambda t: (0, w), pipeline_mode=pl.Buffered(1))
    block = pl.BlockSpec((sources, channels_each, tile), lambda t: (0, 0, t))
    return pl.pallas_call(
        mlp_kernel,
        grid=(count // tile,),
        in_specs=[block, whole((channels, 1)), weight(0), weight(1), weight(2)],
        out_specs=block,
        out_shape=jax.ShapeDtypeStruct(tokens.shape, BF16),
        scratch_shapes=[pltpu.VMEM((channels, hidden_units), BF16)],
        compiler_params=params(48),
        name="mlp",
    )(tokens, norm_gain.reshape(channels, 1), weights, weights, weights)


def gather_weights(w_gate, w_up, w_down, lines):
    half = w_gate.shape[0] // 2
    start = lax.axis_index("core") * half
    mine = jnp.concatenate(
        [lax.dynamic_slice_in_dim(w, start, half, 0) for w in (w_gate, w_up, w_down)], axis=1
    )
    pieces = [mine] + [
        lax.ppermute(mine, "zl", [(i, i ^ d) for i in range(lines)]) for d in range(1, lines)
    ]
    return lax.all_gather(jnp.concatenate(pieces, axis=0), ("y", "core"), axis=0, tiled=True)


def exchange(value, axes):
    return lax.all_to_all(value, axes, split_axis=0, concat_axis=0, tiled=True)


def shards(
    inputs,
    kernel,
    forward_one,
    forward_two,
    inverse_one,
    inverse_two,
    norm_gain,
    w_gate,
    w_up,
    w_down,
    lines,
):
    channels = inputs.shape[0]
    weights = gather_weights(w_gate, w_up, w_down, lines)
    sections = first_sections(inputs, forward_one).reshape(16, 32, channels * 32)
    parts = partial_inverses(exchange(sections, SEQ_AXES), kernel, forward_two, inverse_two)
    parts = exchange(parts.reshape(16, 32, channels * 32), SEQ_AXES)
    tokens = exchange(residuals(parts, inputs, inverse_one), CHAN_AXES)
    result = exchange(mlp(tokens, norm_gain, weights), CHAN_AXES)
    return result.transpose(1, 0, 2).reshape(inputs.shape)


def solution(mesh):
    fine = Mesh(mesh.devices.reshape(2, 4, 2, 4, 4), ("zh", "x", "core", "y", "zl"))
    return jax.shard_map(
        functools.partial(shards, lines=4),
        mesh=fine,
        in_specs=(
            P(CHAN_AXES, SEQ_AXES),
            P(CHAN_AXES, SEQ_AXES, None),
            P(),
            P(),
            P(),
            P(),
            P(),
            P(CHAN_AXES, None),
            P(CHAN_AXES, None),
            P(CHAN_AXES, None),
        ),
        out_specs=P(CHAN_AXES, SEQ_AXES),
        check_vma=False,
    )
```

```python
import functools

import jax
import jax.numpy as jnp
from jax import lax
from jax.experimental import pallas as pl
from jax.experimental.pallas import tpu as pltpu
from jax.sharding import Mesh
from jax.sharding import PartitionSpec as P

SEQ_AXES = ("zh", "x", "core")
CHAN_AXES = ("y", "zl")
F32 = jnp.float32
BF16 = jnp.bfloat16
NT = (((1,), (1,)), ((), ()))
NN = (((1,), (0,)), ((), ()))


def params(mib):
    return pltpu.CompilerParams(vmem_limit_bytes=mib << 20)


def in_hbm(*values):
    return [pltpu.with_memory_space_constraint(value, pltpu.HBM) for value in values]


def whole(shape):
    return pl.BlockSpec(shape, lambda *_: (0,) * len(shape), pipeline_mode=pl.Buffered(1))


def swap_matrix(n):
    r = lax.broadcasted_iota(jnp.int32, (n * n, n * n), 0)
    c = lax.broadcasted_iota(jnp.int32, (n * n, n * n), 1)
    return ((r // n == c % n) & (r % n == c // n)).astype(F32).astype(BF16)


def chunk_matrix(n, width):
    size = n * n * width
    r = lax.broadcasted_iota(jnp.int32, (size, size), 0)
    c = lax.broadcasted_iota(jnp.int32, (size, size), 1)
    ri, rj, rl = r // (n * width), (r // width) % n, r % width
    ci, cj, cl = c // (n * width), (c // width) % n, c % width
    return ((ri == cj) & (rj == ci) & (rl == cl)).astype(F32).astype(BF16)


def dot(a, b, dims=NN):
    return lax.dot_general(a, b, dims, preferred_element_type=F32)


def section_kernel(x_ref, factor_ref, out_ref, swap, turned, rows):
    @pl.when(pl.program_id(0) == 0)
    def _():
        swap[...] = swap_matrix(16)
        turned[...] = factor_ref[...].astype(F32).T.astype(BF16)

    for half in range(2):
        stack = jnp.concatenate(
            [x_ref[:, (half * 16 + a) * 512 : (half * 16 + a + 1) * 512] for a in range(16)], axis=0
        )
        moved = dot(swap[...], stack).astype(BF16)
        for c in range(16):
            rows[c * 32 + half * 16 : c * 32 + half * 16 + 16, :] = moved[c * 16 : c * 16 + 16]
    out_ref[...] = dot(turned[...], rows[...], NT).astype(BF16)


def first_sections(inputs, forward_one):
    channels, positions = inputs.shape
    return pl.pallas_call(
        section_kernel,
        grid=(channels // 16,),
        in_specs=[pl.BlockSpec((16, positions), lambda g: (g, 0)), whole((512, 512))],
        out_specs=pl.BlockSpec((512, 512), lambda g: (0, g)),
        out_shape=jax.ShapeDtypeStruct((512, channels * 32), BF16),
        scratch_shapes=[
            pltpu.VMEM((256, 256), BF16),
            pltpu.VMEM((512, 512), BF16),
            pltpu.VMEM((512, 512), BF16),
        ],
        compiler_params=params(32),
        name="first_sections",
    )(*in_hbm(inputs, forward_one))


def gather_rows(in_ref, chunks, rows):
    for tile in range(2):
        lanes = slice(tile * 128, tile * 128 + 128)
        stack = jnp.concatenate(
            [
                jnp.concatenate([in_ref[4 * g + i, :, lanes] for i in range(4)], axis=1)
                for g in range(4)
            ],
            axis=0,
        )
        moved = dot(stack, chunks[...]).astype(BF16)
        for j in range(4):
            for g in range(4):
                rows[(tile * 4 + j) * 32 : (tile * 4 + j) * 32 + 32, g * 128 : g * 128 + 128] = moved[
                    g * 32 : g * 32 + 32, j * 128 : j * 128 + 128
                ]


def spectrum_kernel(in_ref, kernel_ref, forward_ref, inverse_ref, out_ref, chunks, turned, rows):
    @pl.when(pl.program_id(0) == 0)
    def _():
        chunks[...] = chunk_matrix(4, 32)
        turned[...] = inverse_ref[...].astype(F32).T.astype(BF16)

    gather_rows(in_ref, chunks, rows)
    spectrum = dot(rows[...], forward_ref[...])
    scaled = (spectrum * kernel_ref[...].reshape(256, 512).astype(F32)).astype(BF16)
    out_ref[...] = dot(turned[...], scaled, NT).astype(BF16)


def partial_inverses(sections, kernel, forward_two, inverse_two):
    channels = kernel.shape[0]
    return pl.pallas_call(
        spectrum_kernel,
        grid=(channels // 8,),
        in_specs=[
            pl.BlockSpec((16, 32, 256), lambda g: (0, 0, g)),
            pl.BlockSpec((8, 32, 512), lambda g: (g, 0, 0)),
            whole((512, 512)),
            whole((512, 512)),
        ],
        out_specs=pl.BlockSpec((512, 256), lambda g: (0, g)),
        out_shape=jax.ShapeDtypeStruct((512, channels * 32), BF16),
        scratch_shapes=[
            pltpu.VMEM((512, 512), BF16),
            pltpu.VMEM((512, 512), BF16),
            pltpu.VMEM((256, 512), BF16),
        ],
        compiler_params=params(32),
        name="partial_inverses",
    )(sections, *in_hbm(kernel, forward_two, inverse_two))


def resid_kernel(in_ref, x_ref, inverse_ref, out_ref, chunks, swap, rows, total):
    @pl.when(pl.program_id(0) == 0)
    def _():
        chunks[...] = chunk_matrix(4, 32)
        swap[...] = swap_matrix(16)

    for half in range(2):
        stack = jnp.concatenate(
            [x_ref[:, (half * 16 + i) * 512 : (half * 16 + i + 1) * 512] for i in range(16)], axis=0
        )
        moved = dot(swap[...], stack)
        for c in range(16):
            total[c * 32 + half * 16 : c * 32 + half * 16 + 16, :] = moved[c * 16 : c * 16 + 16]
    for part in range(2):
        gather_rows(in_ref.at[:, :, part * 256 : part * 256 + 256], chunks, rows)
        here = slice(part * 256, part * 256 + 256)
        total[here, :] = total[here, :] + dot(rows[...], inverse_ref[...])
    for half in range(2):
        stack = jnp.concatenate(
            [total[c * 32 + half * 16 : c * 32 + half * 16 + 16, :] for c in range(16)], axis=0
        )
        moved = dot(swap[...], stack.astype(BF16)).astype(BF16)
        for a in range(16):
            i = half * 16 + a
            out_ref[i // 2, :, (i % 2) * 512 : (i % 2) * 512 + 512] = moved[a * 16 : a * 16 + 16]


def residuals(parts, inputs, inverse_one):
    channels, positions = inputs.shape
    return pl.pallas_call(
        resid_kernel,
        grid=(channels // 16,),
        in_specs=[
            pl.BlockSpec((16, 32, 512), lambda g: (0, 0, g)),
            pl.BlockSpec((16, positions), lambda g: (g, 0)),
            whole((512, 512)),
        ],
        out_specs=pl.BlockSpec((16, 16, 1024), lambda g: (0, g, 0)),
        out_shape=jax.ShapeDtypeStruct((16, channels, positions // 16), BF16),
        scratch_shapes=[
            pltpu.VMEM((512, 512), BF16),
            pltpu.VMEM((256, 256), BF16),
            pltpu.VMEM((256, 512), BF16),
            pltpu.VMEM((512, 512), F32),
        ],
        compiler_params=params(32),
        name="residuals",
    )(parts, *in_hbm(inputs, inverse_one))


def layout_kernel(core_ref, *refs):
    pieces, (gate_ref, up_ref, down_ref) = refs[:-3], refs[-3:]
    count = len(pieces) // 2
    rows, columns = pieces[0].shape
    channels, odd = 2 * columns // 3, columns // 3

    def emit(lefts, rights):
        for n, (left, right) in enumerate(zip(lefts, rights)):
            here = slice(n * rows, n * rows + rows)
            gate_ref[here, :] = left[:, :channels]
            up_ref[here, :odd] = left[:, channels:]
            up_ref[here, odd:] = right[:, :odd]
            down_ref[:, here] = right[:, odd:].astype(F32).T.astype(BF16)

    @pl.when(core_ref[0] == 0)
    def _():
        emit(pieces[:count], pieces[count:])

    @pl.when(core_ref[0] == 1)
    def _():
        emit(pieces[count:], pieces[:count])


def lay_out(core, mine, others):
    rows, columns = mine[0].shape
    channels, hidden_units = 2 * columns // 3, rows * len(mine)
    pieces = [*mine, *others]
    return pl.pallas_call(
        layout_kernel,
        in_specs=[pl.BlockSpec(memory_space=pltpu.SMEM)] + [whole((rows, columns))] * len(pieces),
        grid=(1,),
        out_specs=[
            whole((hidden_units, channels)),
            whole((hidden_units, channels)),
            whole((channels, hidden_units)),
        ],
        out_shape=[
            jax.ShapeDtypeStruct((hidden_units, channels), BF16),
            jax.ShapeDtypeStruct((hidden_units, channels), BF16),
            jax.ShapeDtypeStruct((channels, hidden_units), BF16),
        ],
        compiler_params=params(40),
        cost_estimate=pl.CostEstimate(flops=0, bytes_accessed=12 * rows * columns * len(pieces), transcendentals=0),
        name="lay_out_weights",
    )(core.reshape(1), *pieces)


def mlp_kernel(x_ref, gain_ref, gate_ref, up_ref, down_ref, out_ref, normed, total):
    channels, width = normed.shape
    part = pl.program_id(0)

    @pl.when(part == 0)
    def _():
        stream = x_ref[...].reshape(channels, width).astype(F32)
        mean_square = jnp.mean(stream * stream, axis=0, keepdims=True)
        normed[...] = (stream * lax.rsqrt(mean_square + 1e-05) * gain_ref[...]).astype(BF16)
        total[...] = stream

    for t in range(0, width, 512):
        here = slice(t, t + 512)
        gate_part = dot(gate_ref[...], normed[:, here])
        up_part = dot(up_ref[...], normed[:, here])
        curve = 0.7978845608 * (gate_part + 0.044715 * gate_part * gate_part * gate_part)
        hidden = (0.5 * gate_part * (1.0 + jnp.tanh(curve)) * up_part).astype(BF16)
        total[:, here] = total[:, here] + dot(down_ref[...], hidden)

    @pl.when(part == pl.num_programs(0) - 1)
    def _():
        out_ref[...] = total[...].astype(BF16).reshape(out_ref.shape)


def mlp(tokens, norm_gain, weights):
    sources, channels_each, count = tokens.shape
    channels = sources * channels_each
    hidden_units = weights[0].shape[0]
    step = 512
    return pl.pallas_call(
        mlp_kernel,
        grid=(hidden_units // step,),
        in_specs=[
            whole(tokens.shape),
            whole((channels, 1)),
            pl.BlockSpec((step, channels), lambda h: (h, 0)),
            pl.BlockSpec((step, channels), lambda h: (h, 0)),
            pl.BlockSpec((channels, step), lambda h: (0, h)),
        ],
        out_specs=whole(tokens.shape),
        out_shape=jax.ShapeDtypeStruct(tokens.shape, BF16),
        scratch_shapes=[pltpu.VMEM((channels, count), BF16), pltpu.VMEM((channels, count), F32)],
        compiler_params=params(40),
        name="mlp",
    )(tokens, norm_gain.reshape(channels, 1), *in_hbm(*weights))


def pack(w_gate, w_up, w_down, core):
    rows, odd = w_gate.shape[0] // 4, w_up.shape[1] // 2
    start = lax.axis_index("x") * rows
    gate, up, down = (lax.dynamic_slice_in_dim(w, start, rows, 0) for w in (w_gate, w_up, w_down))
    left = jnp.concatenate([gate, up[:, :odd]], axis=1)
    right = jnp.concatenate([up[:, odd:], down], axis=1)
    return jnp.where(core == 0, left, right)


def with_partners(value, axis, size):
    return [value] + [
        lax.ppermute(value, axis, [(i, i ^ d) for i in range(size)]) for d in range(1, size)
    ]


def exchange(value, axes):
    return lax.all_to_all(value, axes, split_axis=0, concat_axis=0, tiled=True)


def shards(
    inputs,
    kernel,
    forward_one,
    forward_two,
    inverse_one,
    inverse_two,
    norm_gain,
    w_gate,
    w_up,
    w_down,
    lines,
):
    channels = inputs.shape[0]
    core = lax.axis_index("core")
    lined = with_partners(pack(w_gate, w_up, w_down, core), "zl", lines)
    sections = first_sections(inputs, forward_one).reshape(16, 32, channels * 32)
    sections, lined = lax.optimization_barrier((sections, lined))
    line = jnp.concatenate(lined, axis=0)
    half = line.shape[0] // 2
    first = [with_partners(line[:half], "x", lines), with_partners(line[half:], "y", lines)]
    sections, first = lax.optimization_barrier((exchange(sections, SEQ_AXES), first))
    pieces = with_partners(jnp.concatenate(first[0], axis=0), "y", lines)
    pieces += with_partners(jnp.concatenate(first[1], axis=0), "x", lines)
    parts = partial_inverses(sections, kernel, forward_two, inverse_two)
    parts = exchange(parts.reshape(16, 32, channels * 32), SEQ_AXES)
    parts, pieces = lax.optimization_barrier((parts, pieces))
    others = [lax.ppermute(piece, "core", [(0, 1), (1, 0)]) for piece in pieces]
    tokens = exchange(residuals(parts, inputs, inverse_one), CHAN_AXES)
    weights = lay_out(core, pieces, others)
    result = exchange(mlp(tokens, norm_gain, weights), CHAN_AXES)
    return result.transpose(1, 0, 2).reshape(inputs.shape)


def solution(mesh):
    fine = Mesh(mesh.devices.reshape(2, 4, 2, 4, 4), ("zh", "x", "core", "y", "zl"))
    return jax.shard_map(
        functools.partial(shards, lines=4),
        mesh=fine,
        in_specs=(
            P(CHAN_AXES, SEQ_AXES),
            P(CHAN_AXES, SEQ_AXES, None),
            P(),
            P(),
            P(),
            P(),
            P(),
            P(CHAN_AXES, None),
            P(CHAN_AXES, None),
            P(CHAN_AXES, None),
        ),
        out_specs=P(CHAN_AXES, SEQ_AXES),
        check_vma=False,
    )
```

```python
import functools

import jax
import jax.numpy as jnp
import numpy as np
from jax import lax
from jax.experimental import pallas as pl
from jax.experimental.pallas import tpu as pltpu
from jax.sharding import Mesh
from jax.sharding import PartitionSpec as P

SEQ_AXES = ("zh", "x", "core")
CHAN_AXES = ("y", "zl")
F32 = jnp.float32
BF16 = jnp.bfloat16
NT = (((1,), (1,)), ((), ()))
NN = (((1,), (0,)), ((), ()))


def params(mib):
    return pltpu.CompilerParams(vmem_limit_bytes=mib << 20)


def in_hbm(*values):
    return [pltpu.with_memory_space_constraint(value, pltpu.HBM) for value in values]


def whole(shape):
    return pl.BlockSpec(shape, lambda *_: (0,) * len(shape), pipeline_mode=pl.Buffered(1))


def swap_matrix(n):
    r = np.arange(n * n)
    return jnp.asarray(np.eye(n * n)[(r % n) * n + r // n], BF16)


def dot(a, b, dims=NN):
    return lax.dot_general(a, b, dims, preferred_element_type=F32)


def swapped(blocks, swap_ref):
    moved = dot(swap_ref[...], jnp.concatenate(blocks, axis=0)).astype(BF16)
    return [moved[n * 16 : n * 16 + 16] for n in range(16)]


def section_kernel(x_ref, factor_ref, swap_ref, out_ref, turned):
    @pl.when(pl.program_id(0) == 0)
    def _():
        turned[...] = factor_ref[...].astype(F32).T.astype(BF16)

    for n in range(0, x_ref.shape[0], 16):
        halves = [
            swapped([x_ref[n : n + 16, a * 512 : a * 512 + 512] for a in range(h, h + 16)], swap_ref)
            for h in (0, 16)
        ]
        rows = jnp.concatenate([half[c] for c in range(16) for half in halves], axis=0)
        out_ref[:, n * 32 : n * 32 + 512] = dot(turned[...], rows, NT).astype(BF16)


def first_sections(inputs, forward_one):
    channels, positions = inputs.shape
    return pl.pallas_call(
        section_kernel,
        grid=(channels // 48,),
        in_specs=[
            pl.BlockSpec((48, positions), lambda g: (g, 0)),
            whole((512, 512)),
            whole((256, 256)),
        ],
        out_specs=pl.BlockSpec((512, 48 * 32), lambda g: (0, g)),
        out_shape=jax.ShapeDtypeStruct((512, channels * 32), BF16),
        scratch_shapes=[pltpu.VMEM((512, 512), BF16)],
        compiler_params=params(32),
        name="first_sections",
    )(*in_hbm(inputs, forward_one, swap_matrix(16)))


def gathered(in_ref, tiles):
    chunk = lax.broadcasted_iota(jnp.int32, (128, 128), 1) // 32
    masks = [chunk == i for i in range(4)]
    rows = []
    for t in tiles:
        parts = [
            jnp.concatenate(
                [in_ref[4 * g + i, :, t * 128 : t * 128 + 128] for g in range(4)], axis=0
            )
            for i in range(4)
        ]
        for j in range(4):
            out = parts[j]
            for i in range(4):
                if i != j:
                    out = jnp.where(masks[i], pltpu.roll(parts[i], (i - j) % 4 * 32, axis=1), out)
            rows.append(jnp.concatenate([out[g * 32 : g * 32 + 32] for g in range(4)], axis=1))
    return jnp.concatenate(rows, axis=0)


def spectrum_kernel(in_ref, kernel_ref, forward_ref, turned_ref, out_ref):
    channels = kernel_ref.shape[0]
    for c in range(0, channels, 8):
        rows = gathered(in_ref, (c // 4, c // 4 + 1))
        spectrum = dot(rows, forward_ref[...])
        scaled = (spectrum * kernel_ref[c : c + 8].reshape(256, 512).astype(F32)).astype(BF16)
        out_ref[:, c * 32 : c * 32 + 256] = dot(turned_ref[...], scaled, NT).astype(BF16)


def partial_inverses(sections, kernel, forward_two, turned_two):
    channels, step = kernel.shape[0], 48
    return pl.pallas_call(
        spectrum_kernel,
        grid=(channels // step,),
        in_specs=[
            pl.BlockSpec((16, 32, step * 32), lambda g: (0, 0, g)),
            pl.BlockSpec((step, 32, 512), lambda g: (g, 0, 0)),
            whole((512, 512)),
            whole((512, 512)),
        ],
        out_specs=pl.BlockSpec((512, step * 32), lambda g: (0, g)),
        out_shape=jax.ShapeDtypeStruct((512, channels * 32), BF16),
        compiler_params=params(32),
        name="partial_inverses",
    )(sections, *in_hbm(kernel, forward_two, turned_two))


def resid_kernel(in_ref, x_ref, inverse_ref, swap_ref, out_ref):
    for first in range(0, x_ref.shape[0], 16):
        here = slice(first, first + 16)
        halves = [
            swapped([x_ref[here, i * 512 : i * 512 + 512] for i in range(h, h + 16)], swap_ref)
            for h in (0, 16)
        ]
        resid = []
        for c in range(0, 16, 8):
            tile = (first + c) // 4
            mixed = dot(gathered(in_ref, (tile, tile + 1)), inverse_ref[...])
            x = jnp.concatenate([half[n] for n in range(c, c + 8) for half in halves], axis=0)
            resid.append((x.astype(F32) + mixed).astype(BF16))
        for h in range(2):
            blocks = [
                resid[c // 8][(c % 8) * 32 + h * 16 : (c % 8) * 32 + h * 16 + 16] for c in range(16)
            ]
            for n, block in enumerate(swapped(blocks, swap_ref)):
                i = h * 16 + n
                out_ref[i // 2, here, (i % 2) * 512 : (i % 2) * 512 + 512] = block


def residuals(parts, inputs, inverse_one):
    channels, positions = inputs.shape
    return pl.pallas_call(
        resid_kernel,
        grid=(channels // 48,),
        in_specs=[
            pl.BlockSpec((16, 32, 48 * 32), lambda g: (0, 0, g)),
            pl.BlockSpec((48, positions), lambda g: (g, 0)),
            whole((512, 512)),
            whole((256, 256)),
        ],
        out_specs=pl.BlockSpec((16, 48, 1024), lambda g: (0, g, 0)),
        out_shape=jax.ShapeDtypeStruct((16, channels, positions // 16), BF16),
        compiler_params=params(32),
        name="residuals",
    )(parts, *in_hbm(inputs, inverse_one, swap_matrix(16)))


def layout_kernel(core_ref, *refs):
    pieces, (gate_ref, up_ref, down_ref) = refs[:-3], refs[-3:]
    count = len(pieces) // 2
    rows, columns = pieces[0].shape
    channels, odd = 2 * columns // 3, columns // 3

    def emit(lefts, rights):
        for n, (left, right) in enumerate(zip(lefts, rights)):
            here = slice(n * rows, n * rows + rows)
            gate_ref[here, :] = left[:, :channels]
            up_ref[here, :odd] = left[:, channels:]
            up_ref[here, odd:] = right[:, :odd]
            down_ref[:, here] = right[:, odd:].astype(F32).T.astype(BF16)

    @pl.when(core_ref[0] == 0)
    def _():
        emit(pieces[:count], pieces[count:])

    @pl.when(core_ref[0] == 1)
    def _():
        emit(pieces[count:], pieces[:count])


def lay_out(core, mine, others):
    rows, columns = mine[0].shape
    channels, hidden_units = 2 * columns // 3, rows * len(mine)
    pieces = [*mine, *others]
    return pl.pallas_call(
        layout_kernel,
        in_specs=[pl.BlockSpec(memory_space=pltpu.SMEM)] + [whole((rows, columns))] * len(pieces),
        grid=(1,),
        out_specs=[
            whole((hidden_units, channels)),
            whole((hidden_units, channels)),
            whole((channels, hidden_units)),
        ],
        out_shape=[
            jax.ShapeDtypeStruct((hidden_units, channels), BF16),
            jax.ShapeDtypeStruct((hidden_units, channels), BF16),
            jax.ShapeDtypeStruct((channels, hidden_units), BF16),
        ],
        compiler_params=params(40),
        cost_estimate=pl.CostEstimate(flops=0, bytes_accessed=12 * rows * columns * len(pieces), transcendentals=0),
        name="lay_out_weights",
    )(core.reshape(1), *pieces)


def mlp_kernel(x_ref, gain_ref, gate_hbm, up_hbm, down_hbm, out_ref, gate, up, down, sems, normed):
    hidden_units, channels = gate.shape
    width = normed.shape[1]
    step = hidden_units // 3
    copies = []
    for n in range(3):
        here = pl.ds(n * step, step)
        copies.append(
            [
                pltpu.make_async_copy(gate_hbm.at[here, :], gate.at[here, :], sems.at[n, 0]),
                pltpu.make_async_copy(up_hbm.at[here, :], up.at[here, :], sems.at[n, 1]),
                pltpu.make_async_copy(down_hbm.at[:, here], down.at[:, here], sems.at[n, 2]),
            ]
        )
    for group in copies:
        for copy in group:
            copy.start()
    for t in range(0, width, 1024):
        tokens = slice(t, t + 1024)
        stream = x_ref[:, :, tokens].reshape(channels, 1024).astype(F32)
        mean_square = jnp.mean(stream * stream, axis=0, keepdims=True)
        normed[:, tokens] = (stream * lax.rsqrt(mean_square + 1e-05) * gain_ref[...]).astype(BF16)
    for t in range(0, width, 1024):
        tokens = slice(t, t + 1024)
        total = x_ref[:, :, tokens].reshape(channels, 1024).astype(F32)
        for n in range(3):
            if t == 0:
                for copy in copies[n]:
                    copy.wait()
            here = slice(n * step, n * step + step)
            gate_part = dot(gate[here, :], normed[:, tokens])
            up_part = dot(up[here, :], normed[:, tokens])
            curve = gate_part * (0.7978845608 + (0.7978845608 * 0.044715) * (gate_part * gate_part))
            half = 0.5 * gate_part
            hidden = ((half + half * jnp.tanh(curve)) * up_part).astype(BF16)
            total = total + dot(down[:, here], hidden)
        out_ref[:, :, tokens] = total.astype(BF16).reshape(out_ref.shape[0], out_ref.shape[1], 1024)


def mlp(tokens, norm_gain, weights):
    sources, channels_each, count = tokens.shape
    channels = sources * channels_each
    hidden_units = weights[0].shape[0]
    anywhere = pl.BlockSpec(memory_space=pl.ANY)
    return pl.pallas_call(
        mlp_kernel,
        in_specs=[
            pl.BlockSpec(memory_space=pltpu.VMEM),
            pl.BlockSpec(memory_space=pltpu.VMEM),
            anywhere,
            anywhere,
            anywhere,
        ],
        out_specs=pl.BlockSpec(memory_space=pltpu.VMEM),
        out_shape=jax.ShapeDtypeStruct(tokens.shape, BF16),
        scratch_shapes=[
            pltpu.VMEM((hidden_units, channels), BF16),
            pltpu.VMEM((hidden_units, channels), BF16),
            pltpu.VMEM((channels, hidden_units), BF16),
            pltpu.SemaphoreType.DMA((3, 3)),
            pltpu.VMEM((channels, count), BF16),
        ],
        compiler_params=params(40),
        name="mlp",
    )(tokens, norm_gain.reshape(channels, 1), *in_hbm(*weights))


def pack(w_gate, w_up, w_down, core):
    rows, odd = w_gate.shape[0] // 4, w_up.shape[1] // 2
    start = lax.axis_index("x") * rows
    gate, up, down = (lax.dynamic_slice_in_dim(w, start, rows, 0) for w in (w_gate, w_up, w_down))
    left = jnp.concatenate([gate, up[:, :odd]], axis=1)
    right = jnp.concatenate([up[:, odd:], down], axis=1)
    return jnp.where(core == 0, left, right)


def with_partners(value, axis, size):
    return [value] + [
        lax.ppermute(value, axis, [(i, i ^ d) for i in range(size)]) for d in range(1, size)
    ]


def exchange(value, axes):
    return lax.all_to_all(value, axes, split_axis=0, concat_axis=0, tiled=True)


def shards(
    inputs,
    kernel,
    forward_one,
    forward_two,
    inverse_one,
    inverse_two,
    norm_gain,
    w_gate,
    w_up,
    w_down,
    lines,
):
    channels = inputs.shape[0]
    core = lax.axis_index("core")
    lined = with_partners(pack(w_gate, w_up, w_down, core), "zl", lines)
    sections = first_sections(inputs, forward_one).reshape(16, 32, channels * 32)
    sections, lined = lax.optimization_barrier((sections, lined))
    line = jnp.concatenate(lined, axis=0)
    half = line.shape[0] // 2
    first = [with_partners(line[:half], "x", lines), with_partners(line[half:], "y", lines)]
    sections, first = lax.optimization_barrier((exchange(sections, SEQ_AXES), first))
    pieces = with_partners(jnp.concatenate(first[0], axis=0), "y", lines)
    pieces += with_partners(jnp.concatenate(first[1], axis=0), "x", lines)
    parts = partial_inverses(sections, kernel, forward_two, inverse_two.T)
    parts = exchange(parts.reshape(16, 32, channels * 32), SEQ_AXES)
    parts, pieces = lax.optimization_barrier((parts, pieces))
    others = [lax.ppermute(piece, "core", [(0, 1), (1, 0)]) for piece in pieces]
    tokens = exchange(residuals(parts, inputs, inverse_one), CHAN_AXES)
    weights = lay_out(core, pieces, others)
    result = exchange(mlp(tokens, norm_gain, weights), CHAN_AXES)
    return result.transpose(1, 0, 2).reshape(inputs.shape)


def solution(mesh):
    fine = Mesh(mesh.devices.reshape(2, 4, 2, 4, 4), ("zh", "x", "core", "y", "zl"))
    return jax.shard_map(
        functools.partial(shards, lines=4),
        mesh=fine,
        in_specs=(
            P(CHAN_AXES, SEQ_AXES),
            P(CHAN_AXES, SEQ_AXES, None),
            P(),
            P(),
            P(),
            P(),
            P(),
            P(CHAN_AXES, None),
            P(CHAN_AXES, None),
            P(CHAN_AXES, None),
        ),
        out_specs=P(CHAN_AXES, SEQ_AXES),
        check_vma=False,
    )
```

```python
import functools

import jax
import jax.numpy as jnp
import numpy as np
from jax import lax
from jax.experimental import pallas as pl
from jax.experimental.pallas import tpu as pltpu
from jax.sharding import Mesh
from jax.sharding import PartitionSpec as P

SEQ_AXES = ("zh", "x", "core")
CHAN_AXES = ("y", "zl")
F32 = jnp.float32
BF16 = jnp.bfloat16
NT = (((1,), (1,)), ((), ()))
NN = (((1,), (0,)), ((), ()))


def params(mib):
    return pltpu.CompilerParams(vmem_limit_bytes=mib << 20)


def in_hbm(*values):
    return [pltpu.with_memory_space_constraint(value, pltpu.HBM) for value in values]


def whole(shape):
    return pl.BlockSpec(shape, lambda *_: (0,) * len(shape), pipeline_mode=pl.Buffered(1))


def swap_matrix(n):
    r = np.arange(n * n)
    return jnp.asarray(np.eye(n * n)[(r % n) * n + r // n], BF16)


def dot(a, b, dims=NN):
    return lax.dot_general(a, b, dims, preferred_element_type=F32)


def swapped(blocks, swap_ref):
    moved = dot(swap_ref[...], jnp.concatenate(blocks, axis=0)).astype(BF16)
    return [moved[n * 16 : n * 16 + 16] for n in range(16)]


def section_kernel(x_ref, factor_ref, swap_ref, out_ref, turned):
    @pl.when(pl.program_id(0) == 0)
    def _():
        turned[...] = factor_ref[...].astype(F32).T.astype(BF16)

    for n in range(0, x_ref.shape[0], 16):
        halves = [
            swapped([x_ref[n : n + 16, a * 512 : a * 512 + 512] for a in range(h, h + 16)], swap_ref)
            for h in (0, 16)
        ]
        rows = jnp.concatenate([half[c] for c in range(16) for half in halves], axis=0)
        out_ref[:, n * 32 : n * 32 + 512] = dot(turned[...], rows, NT).astype(BF16)


def first_sections(inputs, forward_one):
    channels, positions = inputs.shape
    return pl.pallas_call(
        section_kernel,
        grid=(channels // 48,),
        in_specs=[
            pl.BlockSpec((48, positions), lambda g: (g, 0)),
            whole((512, 512)),
            whole((256, 256)),
        ],
        out_specs=pl.BlockSpec((512, 48 * 32), lambda g: (0, g)),
        out_shape=jax.ShapeDtypeStruct((512, channels * 32), BF16),
        scratch_shapes=[pltpu.VMEM((512, 512), BF16)],
        compiler_params=params(32),
        name="first_sections",
    )(*in_hbm(inputs, forward_one, swap_matrix(16)))


def gathered(in_ref, tiles):
    chunk = lax.broadcasted_iota(jnp.int32, (128, 128), 1) // 32
    masks = [chunk == i for i in range(4)]
    rows = []
    for t in tiles:
        parts = [
            jnp.concatenate(
                [in_ref[4 * g + i, :, t * 128 : t * 128 + 128] for g in range(4)], axis=0
            )
            for i in range(4)
        ]
        for j in range(4):
            out = parts[j]
            for i in range(4):
                if i != j:
                    out = jnp.where(masks[i], pltpu.roll(parts[i], (i - j) % 4 * 32, axis=1), out)
            rows.append(jnp.concatenate([out[g * 32 : g * 32 + 32] for g in range(4)], axis=1))
    return jnp.concatenate(rows, axis=0)


def spectrum_kernel(in_ref, kernel_ref, forward_ref, turned_ref, out_ref):
    channels = kernel_ref.shape[0]
    for c in range(0, channels, 8):
        rows = gathered(in_ref, (c // 4, c // 4 + 1))
        spectrum = dot(rows, forward_ref[...])
        scaled = (spectrum * kernel_ref[c : c + 8].reshape(256, 512).astype(F32)).astype(BF16)
        out_ref[:, c * 32 : c * 32 + 256] = dot(turned_ref[...], scaled, NT).astype(BF16)


def partial_inverses(sections, kernel, forward_two, turned_two):
    channels, step = kernel.shape[0], 48
    return pl.pallas_call(
        spectrum_kernel,
        grid=(channels // step,),
        in_specs=[
            pl.BlockSpec((16, 32, step * 32), lambda g: (0, 0, g)),
            pl.BlockSpec((step, 32, 512), lambda g: (g, 0, 0)),
            whole((512, 512)),
            whole((512, 512)),
        ],
        out_specs=pl.BlockSpec((512, step * 32), lambda g: (0, g)),
        out_shape=jax.ShapeDtypeStruct((512, channels * 32), BF16),
        compiler_params=params(32),
        name="partial_inverses",
    )(sections, *in_hbm(kernel, forward_two, turned_two))


def resid_kernel(in_ref, x_ref, inverse_ref, swap_ref, out_ref):
    for first in range(0, x_ref.shape[0], 16):
        here = slice(first, first + 16)
        halves = [
            swapped([x_ref[here, i * 512 : i * 512 + 512] for i in range(h, h + 16)], swap_ref)
            for h in (0, 16)
        ]
        resid = []
        for c in range(0, 16, 8):
            tile = (first + c) // 4
            mixed = dot(gathered(in_ref, (tile, tile + 1)), inverse_ref[...])
            x = jnp.concatenate([half[n] for n in range(c, c + 8) for half in halves], axis=0)
            resid.append((x.astype(F32) + mixed).astype(BF16))
        for h in range(2):
            blocks = [
                resid[c // 8][(c % 8) * 32 + h * 16 : (c % 8) * 32 + h * 16 + 16] for c in range(16)
            ]
            for n, block in enumerate(swapped(blocks, swap_ref)):
                i = h * 16 + n
                out_ref[i // 2, here, (i % 2) * 512 : (i % 2) * 512 + 512] = block


def residuals(parts, inputs, inverse_one):
    channels, positions = inputs.shape
    return pl.pallas_call(
        resid_kernel,
        grid=(channels // 48,),
        in_specs=[
            pl.BlockSpec((16, 32, 48 * 32), lambda g: (0, 0, g)),
            pl.BlockSpec((48, positions), lambda g: (g, 0)),
            whole((512, 512)),
            whole((256, 256)),
        ],
        out_specs=pl.BlockSpec((16, 48, 1024), lambda g: (0, g, 0)),
        out_shape=jax.ShapeDtypeStruct((16, channels, positions // 16), BF16),
        compiler_params=params(32),
        name="residuals",
    )(parts, *in_hbm(inputs, inverse_one, swap_matrix(16)))


def layout_kernel(core_ref, *refs):
    pieces, (gate_ref, up_ref, down_ref) = refs[:-3], refs[-3:]
    count = len(pieces) // 2
    rows, columns = pieces[0].shape
    channels, odd = 2 * columns // 3, columns // 3

    def emit(lefts, rights):
        for n, (left, right) in enumerate(zip(lefts, rights)):
            here = slice(n * rows, n * rows + rows)
            gate_ref[here, :] = left[:, :channels]
            up_ref[here, :odd] = left[:, channels:]
            up_ref[here, odd:] = right[:, :odd]
            down_ref[:, here] = right[:, odd:].astype(F32).T.astype(BF16)

    @pl.when(core_ref[0] == 0)
    def _():
        emit(pieces[:count], pieces[count:])

    @pl.when(core_ref[0] == 1)
    def _():
        emit(pieces[count:], pieces[:count])


def lay_out(core, mine, others):
    rows, columns = mine[0].shape
    channels, hidden_units = 2 * columns // 3, rows * len(mine)
    pieces = [*mine, *others]
    return pl.pallas_call(
        layout_kernel,
        in_specs=[pl.BlockSpec(memory_space=pltpu.SMEM)] + [whole((rows, columns))] * len(pieces),
        grid=(1,),
        out_specs=[
            whole((hidden_units, channels)),
            whole((hidden_units, channels)),
            whole((channels, hidden_units)),
        ],
        out_shape=[
            jax.ShapeDtypeStruct((hidden_units, channels), BF16),
            jax.ShapeDtypeStruct((hidden_units, channels), BF16),
            jax.ShapeDtypeStruct((channels, hidden_units), BF16),
        ],
        compiler_params=params(40),
        cost_estimate=pl.CostEstimate(flops=0, bytes_accessed=12 * rows * columns * len(pieces), transcendentals=0),
        name="lay_out_weights",
    )(core.reshape(1), *pieces)


def mlp_kernel(x_ref, gain_ref, gate_hbm, up_hbm, down_hbm, out_ref, gate, up, down, sems, normed):
    hidden_units, channels = gate.shape
    width = normed.shape[1]
    step = hidden_units // 3
    copies = []
    for n in range(3):
        here = pl.ds(n * step, step)
        copies.append(
            [
                pltpu.make_async_copy(gate_hbm.at[here, :], gate.at[here, :], sems.at[n, 0]),
                pltpu.make_async_copy(up_hbm.at[here, :], up.at[here, :], sems.at[n, 1]),
                pltpu.make_async_copy(down_hbm.at[:, here], down.at[:, here], sems.at[n, 2]),
            ]
        )
    for group in copies:
        for copy in group:
            copy.start()
    for t in range(0, width, 1024):
        tokens = slice(t, t + 1024)
        stream = x_ref[:, :, tokens].reshape(channels, 1024).astype(F32)
        mean_square = jnp.mean(stream * stream, axis=0, keepdims=True)
        normed[:, tokens] = (stream * lax.rsqrt(mean_square + 1e-05) * gain_ref[...]).astype(BF16)
    for t in range(0, width, 1024):
        tokens = slice(t, t + 1024)
        total = x_ref[:, :, tokens].reshape(channels, 1024).astype(F32)
        for n in range(3):
            if t == 0:
                for copy in copies[n]:
                    copy.wait()
            here = slice(n * step, n * step + step)
            gate_part = dot(gate[here, :], normed[:, tokens])
            up_part = dot(up[here, :], normed[:, tokens])
            curve = gate_part * (0.7978845608 + (0.7978845608 * 0.044715) * (gate_part * gate_part))
            half = 0.5 * gate_part
            hidden = ((half + half * jnp.tanh(curve)) * up_part).astype(BF16)
            total = total + dot(down[:, here], hidden)
        out_ref[:, :, tokens] = total.astype(BF16).reshape(out_ref.shape[0], out_ref.shape[1], 1024)


def mlp(tokens, norm_gain, weights):
    sources, channels_each, count = tokens.shape
    channels = sources * channels_each
    hidden_units = weights[0].shape[0]
    anywhere = pl.BlockSpec(memory_space=pl.ANY)
    return pl.pallas_call(
        mlp_kernel,
        in_specs=[
            pl.BlockSpec(memory_space=pltpu.VMEM),
            pl.BlockSpec(memory_space=pltpu.VMEM),
            anywhere,
            anywhere,
            anywhere,
        ],
        out_specs=pl.BlockSpec(memory_space=pltpu.VMEM),
        out_shape=jax.ShapeDtypeStruct(tokens.shape, BF16),
        scratch_shapes=[
            pltpu.VMEM((hidden_units, channels), BF16),
            pltpu.VMEM((hidden_units, channels), BF16),
            pltpu.VMEM((channels, hidden_units), BF16),
            pltpu.SemaphoreType.DMA((3, 3)),
            pltpu.VMEM((channels, count), BF16),
        ],
        compiler_params=params(40),
        name="mlp",
    )(tokens, norm_gain.reshape(channels, 1), *in_hbm(*weights))


def pack(w_gate, w_up, w_down, core):
    rows, odd = w_gate.shape[0] // 4, w_up.shape[1] // 2
    start = lax.axis_index("x") * rows
    gate, up, down = (lax.dynamic_slice_in_dim(w, start, rows, 0) for w in (w_gate, w_up, w_down))
    left = jnp.concatenate([gate, up[:, :odd]], axis=1)
    right = jnp.concatenate([up[:, odd:], down], axis=1)
    return jnp.where(core == 0, left, right)


def with_partners(value, axis, size):
    return [value] + [
        lax.ppermute(value, axis, [(i, i ^ d) for i in range(size)]) for d in range(1, size)
    ]


def exchange(value, axes):
    return lax.all_to_all(value, axes, split_axis=0, concat_axis=0, tiled=True)


def shards(
    inputs,
    kernel,
    forward_one,
    forward_two,
    inverse_one,
    inverse_two,
    norm_gain,
    w_gate,
    w_up,
    w_down,
    lines,
):
    channels = inputs.shape[0]
    core = lax.axis_index("core")
    lined = with_partners(pack(w_gate, w_up, w_down, core), "zl", lines)
    sections = first_sections(inputs, forward_one).reshape(16, 32, channels * 32)
    sections, lined = lax.optimization_barrier((sections, lined))
    line = jnp.concatenate(lined, axis=0)
    half = line.shape[0] // 2
    first = [with_partners(line[:half], "x", lines), with_partners(line[half:], "y", lines)]
    sections, first = lax.optimization_barrier((exchange(sections, SEQ_AXES), first))
    pieces = with_partners(jnp.concatenate(first[0], axis=0), "y", lines)
    pieces += with_partners(jnp.concatenate(first[1], axis=0), "x", lines)
    parts = partial_inverses(sections, kernel, forward_two, inverse_two.T)
    parts = exchange(parts.reshape(16, 32, channels * 32), SEQ_AXES)
    parts, pieces[:6] = lax.optimization_barrier((parts, pieces[:6]))
    others = [lax.ppermute(piece, "core", [(0, 1), (1, 0)]) for piece in pieces]
    tokens = exchange(residuals(parts, inputs, inverse_one), CHAN_AXES)
    weights = lay_out(core, pieces, others)
    result = exchange(mlp(tokens, norm_gain, weights), CHAN_AXES)
    return result.transpose(1, 0, 2).reshape(inputs.shape)


def solution(mesh):
    fine = Mesh(mesh.devices.reshape(2, 4, 2, 4, 4), ("zh", "x", "core", "y", "zl"))
    return jax.shard_map(
        functools.partial(shards, lines=4),
        mesh=fine,
        in_specs=(
            P(CHAN_AXES, SEQ_AXES),
            P(CHAN_AXES, SEQ_AXES, None),
            P(),
            P(),
            P(),
            P(),
            P(),
            P(CHAN_AXES, None),
            P(CHAN_AXES, None),
            P(CHAN_AXES, None),
        ),
        out_specs=P(CHAN_AXES, SEQ_AXES),
        check_vma=False,
    )
```

```python
import functools

import jax
import jax.numpy as jnp
import numpy as np
from jax import lax
from jax.experimental import pallas as pl
from jax.experimental.pallas import tpu as pltpu
from jax.sharding import Mesh
from jax.sharding import PartitionSpec as P

SEQ_AXES = ("zh", "x", "core")
CHAN_AXES = ("y", "zl")
F32 = jnp.float32
BF16 = jnp.bfloat16
NT = (((1,), (1,)), ((), ()))
NN = (((1,), (0,)), ((), ()))


def params(mib):
    return pltpu.CompilerParams(vmem_limit_bytes=mib << 20)


def in_hbm(*values):
    return [pltpu.with_memory_space_constraint(value, pltpu.HBM) for value in values]


def whole(shape):
    return pl.BlockSpec(shape, lambda *_: (0,) * len(shape), pipeline_mode=pl.Buffered(1))


def swap_matrix(n):
    r = np.arange(n * n)
    return jnp.asarray(np.eye(n * n)[(r % n) * n + r // n], BF16)


def dot(a, b, dims=NN):
    return lax.dot_general(a, b, dims, preferred_element_type=F32)


def swapped(blocks, swap_ref):
    moved = dot(swap_ref[...], jnp.concatenate(blocks, axis=0)).astype(BF16)
    return [moved[n * 16 : n * 16 + 16] for n in range(16)]


def section_kernel(x_ref, factor_ref, swap_ref, out_ref, turned):
    @pl.when(pl.program_id(0) == 0)
    def _():
        turned[...] = factor_ref[...].astype(F32).T.astype(BF16)

    for n in range(0, x_ref.shape[0], 16):
        halves = [
            swapped([x_ref[n : n + 16, a * 512 : a * 512 + 512] for a in range(h, h + 16)], swap_ref)
            for h in (0, 16)
        ]
        rows = jnp.concatenate([half[c] for c in range(16) for half in halves], axis=0)
        out_ref[:, n * 32 : n * 32 + 512] = dot(turned[...], rows, NT).astype(BF16)


def first_sections(inputs, forward_one):
    channels, positions = inputs.shape
    return pl.pallas_call(
        section_kernel,
        grid=(channels // 48,),
        in_specs=[
            pl.BlockSpec((48, positions), lambda g: (g, 0)),
            whole((512, 512)),
            whole((256, 256)),
        ],
        out_specs=pl.BlockSpec((512, 48 * 32), lambda g: (0, g)),
        out_shape=jax.ShapeDtypeStruct((512, channels * 32), BF16),
        scratch_shapes=[pltpu.VMEM((512, 512), BF16)],
        compiler_params=params(32),
        name="first_sections",
    )(*in_hbm(inputs, forward_one, swap_matrix(16)))


def gathered(in_ref, tiles):
    chunk = lax.broadcasted_iota(jnp.int32, (128, 128), 1) // 32
    masks = [chunk == i for i in range(4)]
    rows = []
    for t in tiles:
        parts = [
            jnp.concatenate(
                [in_ref[4 * g + i, :, t * 128 : t * 128 + 128] for g in range(4)], axis=0
            )
            for i in range(4)
        ]
        for j in range(4):
            out = parts[j]
            for i in range(4):
                if i != j:
                    out = jnp.where(masks[i], pltpu.roll(parts[i], (i - j) % 4 * 32, axis=1), out)
            rows.append(jnp.concatenate([out[g * 32 : g * 32 + 32] for g in range(4)], axis=1))
    return jnp.concatenate(rows, axis=0)


def spectrum_kernel(in_ref, kernel_ref, forward_ref, turned_ref, out_ref):
    channels = kernel_ref.shape[0]
    for c in range(0, channels, 8):
        rows = gathered(in_ref, (c // 4, c // 4 + 1))
        spectrum = dot(rows, forward_ref[...])
        scaled = (spectrum * kernel_ref[c : c + 8].reshape(256, 512).astype(F32)).astype(BF16)
        out_ref[:, c * 32 : c * 32 + 256] = dot(turned_ref[...], scaled, NT).astype(BF16)


def partial_inverses(sections, kernel, forward_two, turned_two):
    channels, step = kernel.shape[0], 48
    return pl.pallas_call(
        spectrum_kernel,
        grid=(channels // step,),
        in_specs=[
            pl.BlockSpec((16, 32, step * 32), lambda g: (0, 0, g)),
            pl.BlockSpec((step, 32, 512), lambda g: (g, 0, 0)),
            whole((512, 512)),
            whole((512, 512)),
        ],
        out_specs=pl.BlockSpec((512, step * 32), lambda g: (0, g)),
        out_shape=jax.ShapeDtypeStruct((512, channels * 32), BF16),
        compiler_params=params(32),
        name="partial_inverses",
    )(sections, *in_hbm(kernel, forward_two, turned_two))


def resid_kernel(in_ref, x_ref, inverse_ref, swap_ref, out_ref):
    for first in range(0, x_ref.shape[0], 16):
        here = slice(first, first + 16)
        halves = [
            swapped([x_ref[here, i * 512 : i * 512 + 512] for i in range(h, h + 16)], swap_ref)
            for h in (0, 16)
        ]
        resid = []
        for c in range(0, 16, 8):
            tile = (first + c) // 4
            mixed = dot(gathered(in_ref, (tile, tile + 1)), inverse_ref[...])
            x = jnp.concatenate([half[n] for n in range(c, c + 8) for half in halves], axis=0)
            resid.append((x.astype(F32) + mixed).astype(BF16))
        for h in range(2):
            blocks = [
                resid[c // 8][(c % 8) * 32 + h * 16 : (c % 8) * 32 + h * 16 + 16] for c in range(16)
            ]
            for n, block in enumerate(swapped(blocks, swap_ref)):
                i = h * 16 + n
                out_ref[i // 2, here, (i % 2) * 512 : (i % 2) * 512 + 512] = block


def residuals(parts, inputs, inverse_one):
    channels, positions = inputs.shape
    return pl.pallas_call(
        resid_kernel,
        grid=(channels // 48,),
        in_specs=[
            pl.BlockSpec((16, 32, 48 * 32), lambda g: (0, 0, g)),
            pl.BlockSpec((48, positions), lambda g: (g, 0)),
            whole((512, 512)),
            whole((256, 256)),
        ],
        out_specs=pl.BlockSpec((16, 48, 1024), lambda g: (0, g, 0)),
        out_shape=jax.ShapeDtypeStruct((16, channels, positions // 16), BF16),
        compiler_params=params(32),
        name="residuals",
    )(parts, *in_hbm(inputs, inverse_one, swap_matrix(16)))


def layout_kernel(core_ref, *refs):
    pieces, (gate_ref, up_ref, down_ref) = refs[:-3], refs[-3:]
    count = len(pieces) // 2
    rows, columns = pieces[0].shape
    channels, odd = 2 * columns // 3, columns // 3

    def emit(lefts, rights):
        for n, (left, right) in enumerate(zip(lefts, rights)):
            here = slice(n * rows, n * rows + rows)
            gate_ref[here, :] = left[:, :channels]
            up_ref[here, :odd] = left[:, channels:]
            up_ref[here, odd:] = right[:, :odd]
            down_ref[:, here] = right[:, odd:].astype(F32).T.astype(BF16)

    @pl.when(core_ref[0] == 0)
    def _():
        emit(pieces[:count], pieces[count:])

    @pl.when(core_ref[0] == 1)
    def _():
        emit(pieces[count:], pieces[:count])


def lay_out(core, mine, others):
    rows, columns = mine[0].shape
    channels, hidden_units = 2 * columns // 3, rows * len(mine)
    pieces = [*mine, *others]
    return pl.pallas_call(
        layout_kernel,
        in_specs=[pl.BlockSpec(memory_space=pltpu.SMEM)] + [whole((rows, columns))] * len(pieces),
        grid=(1,),
        out_specs=[
            whole((hidden_units, channels)),
            whole((hidden_units, channels)),
            whole((channels, hidden_units)),
        ],
        out_shape=[
            pltpu.HBM((hidden_units, channels), BF16),
            pltpu.HBM((hidden_units, channels), BF16),
            pltpu.HBM((channels, hidden_units), BF16),
        ],
        compiler_params=params(40),
        cost_estimate=pl.CostEstimate(flops=0, bytes_accessed=12 * rows * columns * len(pieces), transcendentals=0),
        name="lay_out_weights",
    )(core.reshape(1), *pieces)


def mlp_kernel(x_ref, gain_ref, gate_hbm, up_hbm, down_hbm, out_ref, gate, up, down, sems, normed):
    hidden_units, channels = gate.shape
    width = normed.shape[1]
    step = hidden_units // 3
    copies = []
    for n in range(3):
        here = pl.ds(n * step, step)
        copies.append(
            [
                pltpu.make_async_copy(gate_hbm.at[here, :], gate.at[here, :], sems.at[n, 0]),
                pltpu.make_async_copy(up_hbm.at[here, :], up.at[here, :], sems.at[n, 1]),
                pltpu.make_async_copy(down_hbm.at[:, here], down.at[:, here], sems.at[n, 2]),
            ]
        )
    for group in copies:
        for copy in group:
            copy.start()
    for t in range(0, width, 1024):
        tokens = slice(t, t + 1024)
        stream = x_ref[:, :, tokens].reshape(channels, 1024).astype(F32)
        mean_square = jnp.mean(stream * stream, axis=0, keepdims=True)
        normed[:, tokens] = (stream * lax.rsqrt(mean_square + 1e-05) * gain_ref[...]).astype(BF16)
    for t in range(0, width, 1024):
        tokens = slice(t, t + 1024)
        total = x_ref[:, :, tokens].reshape(channels, 1024).astype(F32)
        for n in range(3):
            if t == 0:
                for copy in copies[n]:
                    copy.wait()
            here = slice(n * step, n * step + step)
            gate_part = dot(gate[here, :], normed[:, tokens])
            up_part = dot(up[here, :], normed[:, tokens])
            curve = gate_part * (0.7978845608 + (0.7978845608 * 0.044715) * (gate_part * gate_part))
            half = 0.5 * gate_part
            hidden = ((half + half * jnp.tanh(curve)) * up_part).astype(BF16)
            total = total + dot(down[:, here], hidden)
        out_ref[:, :, tokens] = total.astype(BF16).reshape(out_ref.shape[0], out_ref.shape[1], 1024)


def mlp(tokens, norm_gain, weights):
    sources, channels_each, count = tokens.shape
    channels = sources * channels_each
    hidden_units = weights[0].shape[0]
    anywhere = pl.BlockSpec(memory_space=pl.ANY)
    return pl.pallas_call(
        mlp_kernel,
        in_specs=[
            pl.BlockSpec(memory_space=pltpu.VMEM),
            pl.BlockSpec(memory_space=pltpu.VMEM),
            anywhere,
            anywhere,
            anywhere,
        ],
        out_specs=pl.BlockSpec(memory_space=pltpu.VMEM),
        out_shape=jax.ShapeDtypeStruct(tokens.shape, BF16),
        scratch_shapes=[
            pltpu.VMEM((hidden_units, channels), BF16),
            pltpu.VMEM((hidden_units, channels), BF16),
            pltpu.VMEM((channels, hidden_units), BF16),
            pltpu.SemaphoreType.DMA((3, 3)),
            pltpu.VMEM((channels, count), BF16),
        ],
        compiler_params=params(40),
        name="mlp",
    )(tokens, norm_gain.reshape(channels, 1), *in_hbm(*weights))


def pack(w_gate, w_up, w_down, core):
    rows, odd = w_gate.shape[0] // 4, w_up.shape[1] // 2
    start = lax.axis_index("x") * rows
    gate, up, down = (lax.dynamic_slice_in_dim(w, start, rows, 0) for w in (w_gate, w_up, w_down))
    left = jnp.concatenate([gate, up[:, :odd]], axis=1)
    right = jnp.concatenate([up[:, odd:], down], axis=1)
    return jnp.where(core == 0, left, right)


def with_partners(value, axis, size):
    return [value] + [
        lax.ppermute(value, axis, [(i, i ^ d) for i in range(size)]) for d in range(1, size)
    ]


def exchange(value, axes):
    return lax.all_to_all(value, axes, split_axis=0, concat_axis=0, tiled=True)


def shards(
    inputs,
    kernel,
    forward_one,
    forward_two,
    inverse_one,
    inverse_two,
    norm_gain,
    w_gate,
    w_up,
    w_down,
    lines,
):
    channels = inputs.shape[0]
    core = lax.axis_index("core")
    lined = with_partners(pack(w_gate, w_up, w_down, core), "zl", lines)
    sections = first_sections(inputs, forward_one).reshape(16, 32, channels * 32)
    sections, lined = lax.optimization_barrier((sections, lined))
    line = jnp.concatenate(lined, axis=0)
    half = line.shape[0] // 2
    first = [with_partners(line[:half], "x", lines), with_partners(line[half:], "y", lines)]
    sections, first = lax.optimization_barrier((exchange(sections, SEQ_AXES), first))
    pieces = with_partners(jnp.concatenate(first[0], axis=0), "y", lines)
    pieces += with_partners(jnp.concatenate(first[1], axis=0), "x", lines)
    parts = partial_inverses(sections, kernel, forward_two, inverse_two.T)
    parts = exchange(parts.reshape(16, 32, channels * 32), SEQ_AXES)
    parts, pieces[:6] = lax.optimization_barrier((parts, pieces[:6]))
    others = [lax.ppermute(piece, "core", [(0, 1), (1, 0)]) for piece in pieces]
    tokens = exchange(residuals(parts, inputs, inverse_one), CHAN_AXES)
    weights = lay_out(core, pieces, others)
    result = exchange(mlp(tokens, norm_gain, weights), CHAN_AXES)
    return result.transpose(1, 0, 2).reshape(inputs.shape)


def solution(mesh):
    fine = Mesh(mesh.devices.reshape(2, 4, 2, 4, 4), ("zh", "x", "core", "y", "zl"))
    return jax.shard_map(
        functools.partial(shards, lines=4),
        mesh=fine,
        in_specs=(
            P(CHAN_AXES, SEQ_AXES),
            P(CHAN_AXES, SEQ_AXES, None),
            P(),
            P(),
            P(),
            P(),
            P(),
            P(CHAN_AXES, None),
            P(CHAN_AXES, None),
            P(CHAN_AXES, None),
        ),
        out_specs=P(CHAN_AXES, SEQ_AXES),
        check_vma=False,
    )
```
